256 devices in a mesh: wide: 32 (over x, z_lo, core), narrow: 8 (over y, z_hi).
Axes of the slice: x: 4, y: 4, z: 8 (z_hi: 2, z_lo: 4; z = z_hi * 4 + z_lo), core: 2. Of those that a mesh axis runs over, the one named last changes fastest.
Arguments:
- hidden_in: bfloat16 [2048, 6144], P('wide', 'narrow'), may hold values from -6 to 6
- w_query: bfloat16 [6144, 6144], P('narrow', 'wide'), may hold values from -1 to 1
- w_key: bfloat16 [6144, 6144], P('narrow', 'wide'), may hold values from -1 to 1
- w_value: bfloat16 [6144, 6144], P('narrow', 'wide'), may hold values from -0.078125 to 0.078125
- qkv_bias: float32 [3, 6144], P(None, 'wide'), may hold values from -3 to 3
- w_up: bfloat16 [6144, 24576], P('narrow', 'wide'), may hold values from -0.078125 to 0.078125
- up_bias: float32 [24576], P('wide'), may hold values from -3 to 3
- w_attn_out: bfloat16 [6144, 6144], P('wide', 'narrow'), may hold values from -0.078125 to 0.078125
- w_down: bfloat16 [24576, 6144], P('wide', 'narrow'), may hold values from -0.0390625 to 0.0390625
- out_bias: float32 [6144], P('narrow'), may hold values from -3 to 3
- norm_gain: float32 [2, 6144], P(None, 'narrow'), may hold values from 0.5 to 1.5
- norm_bias: float32 [2, 6144], P(None, 'narrow'), may hold values from -2 to 2
- seq_lens: int32 [8], replicated, may hold values from 1 to 1024, 2048 in all
- sink_count: int32 [8], replicated, may hold values from 1 to 64, as said below
- page_table: int32 [128], replicated, may hold values from 0 to 127, each once
Outputs:
- hidden_out: bfloat16 [2048, 6144], P('wide', 'narrow')
- paged_cache: bfloat16 [2, 128, 16, 6144], P(None, 'narrow', None, 'wide')
The draws below stay inside these ranges and needn't reach their ends.
Inputs may be any that keep to these rules, and one draw needn't show every extreme that they name: `seq_lens`: the lengths are positive, add up to 2048, and the longest is exactly 1024. `sink_count`: some sequence has exactly 64 sink tokens. `page_table`: every slot is named by exactly one page.
All inputs are finite; a program needn't handle non-finite values.
Results may differ from the reference program's by a relative error of at most 0.02.
Values may be sent and summed in bfloat16 or wider, within the bound.
A program may use at most 64 MiB of HBM per device.

```python
import math
import jax
import jax.numpy as jnp
import numpy as np
from jax import lax

D = 6144
HEADS = 64
HEAD_DIM = 96
FF = 24576
ROTARY = 24
SEQS = 8
PAGE = 16
TOKENS = 2048
WINDOW = 128
NPAGES = 128
N_NARROW = 8


def sign_vector(key, count):
    return jnp.where(jax.random.normal(key, (count,), jnp.float32) > 0.0, 1.0, -1.0).astype(jnp.float32)


def align_direction(key):
    return sign_vector(jax.random.fold_in(key, 101), D)


def head_pattern(key):
    signs = sign_vector(jax.random.fold_in(key, 102), D)
    column = jnp.arange(D, dtype=jnp.int32)
    kept = (column % HEAD_DIM >= ROTARY).astype(jnp.float32)
    return signs * kept


def strength_factor():
    ratio = (HEAD_DIM - ROTARY) / HEAD_DIM ** 0.5
    return (7.348469 / ratio) ** 0.5


def projection_draw(key, dense, strength):
    direction = align_direction(key)
    pattern = head_pattern(key)
    extra = direction[:, None] * pattern[None, :] * (strength * strength_factor() / D)
    return (dense / D ** 0.5 + extra).astype(jnp.bfloat16)


def draw_w_query(key, part):
    base_key = jax.random.fold_in(key, 201)
    dense = jnp.clip(jax.random.normal(base_key, (D, D), jnp.float32), -6.0, 6.0)
    return projection_draw(key, dense, 12.0)


def draw_w_key(key, part):
    base_key = jax.random.fold_in(key, 202)
    dense = jnp.clip(jax.random.normal(base_key, (D, D), jnp.float32), -6.0, 6.0)
    return projection_draw(key, dense, 3.5)


def draw_hidden_in(key, part):
    picked = jax.random.bernoulli(jax.random.fold_in(key, 301), 1.0 / 16.0, (TOKENS, 1))
    base = jnp.clip(jax.random.normal(jax.random.fold_in(key, 302), (TOKENS, D), jnp.float32), -6.0, 6.0)
    strength = jax.random.uniform(jax.random.fold_in(key, 304), (TOKENS, 1), jnp.float32, 0.75, 0.98)
    direction = align_direction(key)
    aligned = jnp.sqrt(1.0 - strength * strength) * base + strength * direction[None, :]
    column = jnp.arange(D, dtype=jnp.float32) / D
    column_scale = 1.0 + 2.0 * column
    column_offset = column
    drawn = jnp.clip(base * column_scale[None, :] + column_offset[None, :], -6.0, 6.0)
    return jnp.where(picked, aligned, drawn).astype(jnp.bfloat16)


def draw_sink_count(key, part):
    most = WINDOW // 2
    counts = jax.random.randint(jax.random.fold_in(key, 401), (SEQS,), 1, most + 1, jnp.int32)
    chosen = jax.random.randint(jax.random.fold_in(key, 402), (), 0, SEQS, jnp.int32)
    return jnp.where(jnp.arange(SEQS, dtype=jnp.int32) == chosen, jnp.int32(most), counts).astype(jnp.int32)


def level_of(rng, extent, shards, smallest, high):
    factor_of = 1.0
    for dim, shards_of in shards:
        steps = jax.random.uniform(jax.random.fold_in(jax.random.fold_in(rng, 6), dim), (shards_of,), jnp.float32, smallest / len(shards), high / len(shards))
        factor_of = factor_of * jnp.repeat(jnp.exp(steps), extent[dim] // shards_of).reshape((-1,) + (1,) * (len(extent) - 1 - dim))
    return factor_of


def profile(amount, total, limit, lean):
    weights = [(1 << 20) // math.isqrt(standing ** lean) + 1 for standing in range(2, amount + 1)]
    rest, holding = total - limit - (amount - 1), [1] * (amount - 1)
    while rest > 0:
        candidates = [i for i in range(amount - 1) if holding[i] < limit]
        pool, remaining = sum([weights[i] for i in candidates]), rest
        for i in candidates:
            addition = min(limit - holding[i], max(1, remaining * weights[i] // pool), rest)
            holding[i] = holding[i] + addition
            rest = rest - addition
    return np.array([limit] + holding)


def uneven(key, amount, total, bound, slope):
    if amount == 2:
        one = jax.random.randint(key, (), max(1, total - bound), min(bound, total - 1) + 1)
        return jnp.stack([one, total - one])
    sizes = jnp.asarray(profile(amount, total, bound, slope), jnp.int32)
    pairs = (amount - 1) // 2
    giver, receiver = sizes[1:1 + 2 * pairs:2], sizes[2:2 + 2 * pairs:2]
    slack = jnp.minimum(giver - 1, bound - receiver)
    moved = jax.random.randint(jax.random.fold_in(key, 1), (pairs,), 0, 1 << 20) % (slack + 1)
    sizes = sizes.at[1:1 + 2 * pairs:2].set(giver - moved).at[2:2 + 2 * pairs:2].set(receiver + moved)
    return sizes[jax.random.permutation(jax.random.fold_in(key, 2), amount)]


def gaussian(key, shape, width, most, pieces=(), kind=jnp.bfloat16):
    drawn = width * jax.random.normal(key, shape, jnp.float32)
    if pieces:
        drawn = drawn * level_of(key, shape, pieces, -0.22, 0.18)
    return jnp.clip(drawn, -most, most).astype(kind)


def setup_inputs(seed: int = 0) -> dict:
    streams_of = jax.random.split(jax.random.key(seed), 16)
    return {
        "hidden_in": draw_hidden_in(jax.random.fold_in(streams_of[15], 71), 0),
        "w_query": draw_w_query(jax.random.fold_in(streams_of[15], 71), 0),
        "w_key": draw_w_key(jax.random.fold_in(streams_of[15], 71), 0),
        "w_value": gaussian(streams_of[3], (D, D), D ** -0.5, 0.078125, ((0, 8), (1, 32))),
        "qkv_bias": gaussian(streams_of[4], (3, D), 0.5, 3.0, ((1, 32),), jnp.float32),
        "w_up": gaussian(streams_of[5], (D, FF), D ** -0.5, 0.078125, ((0, 8), (1, 32))),
        "up_bias": gaussian(streams_of[6], (FF,), 0.5, 3.0, ((0, 32),), jnp.float32),
        "w_attn_out": gaussian(streams_of[7], (D, D), D ** -0.5, 0.078125, ((0, 32), (1, 8))),
        "w_down": gaussian(streams_of[8], (FF, D), FF ** -0.5, 0.0390625, ((0, 32), (1, 8))),
        "out_bias": gaussian(streams_of[9], (D,), 0.5, 3.0, ((0, 8),), jnp.float32),
        "norm_gain": jnp.clip(1.0 + 0.1 * jax.random.normal(streams_of[10], (2, D), jnp.float32), 0.5, 1.5),
        "norm_bias": gaussian(streams_of[11], (2, D), 0.3, 2.0, ((1, 8),), jnp.float32),
        "seq_lens": uneven(streams_of[12], SEQS, TOKENS, TOKENS // 2, 2).astype(jnp.int32),
        "sink_count": draw_sink_count(jax.random.fold_in(streams_of[15], 71), 0),
        "page_table": jax.random.permutation(streams_of[14], NPAGES).astype(jnp.int32),
    }


def segment_info(token_index, seq_lens, sink_count):
    seq_ends = jnp.cumsum(seq_lens).astype(jnp.int32)
    seq_starts = (seq_ends - seq_lens).astype(jnp.int32)
    inside = (token_index[:, None] >= seq_starts[None, :]) & (token_index[:, None] < seq_ends[None, :])
    member = inside.astype(jnp.int32)
    seq_number = jnp.arange(seq_lens.shape[0], dtype=jnp.int32)
    segment = lax.optimization_barrier(jnp.sum(member * seq_number[None, :], axis=1)).astype(jnp.int32)
    position = (token_index - lax.optimization_barrier(jnp.sum(member * seq_starts[None, :], axis=1))).astype(jnp.int32)
    sink_limit = lax.optimization_barrier(jnp.sum(member * sink_count[None, :], axis=1)).astype(jnp.int32)
    return (segment, position, sink_limit)

def rotate(values, position):
    half_rot = ROTARY // 2
    freq_index = jnp.arange(half_rot, dtype=jnp.float32)
    inverse = jnp.power(jnp.float32(10000.0), -2.0 * freq_index / ROTARY)
    angles = position.astype(jnp.float32)[:, None] * inverse[None, :]
    cosine = jnp.cos(angles)[:, None, :]
    sine_part = jnp.sin(angles)[:, None, :]
    first_half = values[..., :half_rot]
    second_half = values[..., half_rot:ROTARY]
    return jnp.concatenate([first_half * cosine - second_half * sine_part, second_half * cosine + first_half * sine_part, values[..., ROTARY:]], axis=-1)

def blocked(normed, weight):
    width_part = D // N_NARROW
    total = jnp.zeros((normed.shape[0], weight.shape[1]), jnp.float32)
    for block in range(N_NARROW):
        section = normed[:, block * width_part:(block + 1) * width_part].astype(jnp.float32)
        weight_rows = weight[block * width_part:(block + 1) * width_part].astype(jnp.float32)
        partial_term = jnp.dot(section, weight_rows, precision=lax.Precision.HIGHEST).astype(jnp.bfloat16)
        partial_term = lax.optimization_barrier(partial_term)
        total = total + partial_term.astype(jnp.float32)
    return total

def reference(hidden_in, w_query, w_key, w_value, qkv_bias, w_up, up_bias, w_attn_out, w_down, out_bias, norm_gain, norm_bias, seq_lens, sink_count, page_table):
    as_float = hidden_in.astype(jnp.float32)
    average = lax.optimization_barrier(jnp.sum(as_float, axis=1)) / D
    variance = lax.optimization_barrier(jnp.sum(as_float * as_float, axis=1)) / D - average * average
    scaled = (as_float - average[:, None]) * lax.rsqrt(variance + 1e-05)[:, None]
    attn_normed = (scaled * norm_gain[0] + norm_bias[0]).astype(jnp.bfloat16)
    mlp_normed = (scaled * norm_gain[1] + norm_bias[1]).astype(jnp.bfloat16)
    query_sum = blocked(attn_normed, w_query)
    key_sum = blocked(attn_normed, w_key)
    value_sum = blocked(attn_normed, w_value)
    unit_sum = blocked(mlp_normed, w_up)
    token_index = jnp.arange(TOKENS, dtype=jnp.int32)
    segment, position, sink_limit = segment_info(token_index, seq_lens, sink_count)
    queries = rotate((query_sum + qkv_bias[0]).reshape(TOKENS, HEADS, HEAD_DIM), position).astype(jnp.bfloat16)
    keys = rotate((key_sum + qkv_bias[1]).reshape(TOKENS, HEADS, HEAD_DIM), position).astype(jnp.bfloat16)
    values = (value_sum + qkv_bias[2]).astype(jnp.bfloat16).reshape(TOKENS, HEADS, HEAD_DIM)
    hidden_units = jax.nn.gelu(unit_sum + up_bias, approximate=False).astype(jnp.bfloat16)
    allowed = (segment[:, None] == segment[None, :]) & (position[None, :] <= position[:, None])
    allowed = allowed & ((position[:, None] - position[None, :] < WINDOW) | (position[None, :] < sink_limit[:, None]))
    scale = 1.0 / HEAD_DIM ** 0.5

    def one_head(operands):
        query_head, key_head, value_head = operands
        scores = jnp.dot(query_head.astype(jnp.float32), key_head.astype(jnp.float32).T, precision=lax.Precision.HIGHEST) * scale
        masked = jnp.where(allowed, scores, jnp.float32(-1e+30))
        top_score = lax.optimization_barrier(jnp.max(masked, axis=1, keepdims=True))
        weights = jnp.exp(masked - top_score)
        probs = (weights / lax.optimization_barrier(jnp.sum(weights, axis=1, keepdims=True))).astype(jnp.bfloat16)
        return jnp.dot(probs.astype(jnp.float32), value_head.astype(jnp.float32), precision=lax.Precision.HIGHEST).astype(jnp.bfloat16)
    per_head = lax.map(one_head, (jnp.transpose(queries, (1, 0, 2)), jnp.transpose(keys, (1, 0, 2)), jnp.transpose(values, (1, 0, 2))))
    attended = jnp.transpose(per_head, (1, 0, 2)).reshape(TOKENS, D)
    branch_total = jnp.dot(attended.astype(jnp.float32), w_attn_out.astype(jnp.float32), precision=lax.Precision.HIGHEST)
    branch_total = branch_total + jnp.dot(hidden_units.astype(jnp.float32), w_down.astype(jnp.float32), precision=lax.Precision.HIGHEST)
    hidden_out = (as_float + branch_total + out_bias).astype(jnp.bfloat16)
    stacked = jnp.stack([keys.reshape(NPAGES, PAGE, D), values.reshape(NPAGES, PAGE, D)])
    paged_cache = jnp.zeros_like(stacked).at[:, page_table].set(stacked)
    return (hidden_out, paged_cache)
```

```python
import functools

import jax
import jax.numpy as jnp
from jax import lax
from jax.experimental import pallas as pl
from jax.experimental.pallas import tpu as pltpu
from jax.sharding import PartitionSpec as P

D = 6144
HEAD_DIM = 96
ROTARY = 24
PAGE = 16
WINDOW = 128
MOST_SINKS = 64
MESH = pl.DeviceIdType.MESH
F32 = jnp.float32
BF16 = jnp.bfloat16
VM = pltpu.VMEM
DMA = pltpu.SemaphoreType.DMA
QKV_PAD = 640
HALF_FF = 384


class Place:
    def __init__(self):
        wide = lax.axis_index("wide")
        narrow = lax.axis_index("narrow")
        self.x, self.zl, self.c = wide // 8, (wide // 2) % 4, wide % 2
        self.y, self.zh = narrow // 2, narrow % 2
        self.wide, self.narrow = wide, narrow

    def in_wide(self, dx, dz, dc):
        return lax.rem(self.x + dx, 4) * 8 + lax.rem(self.zl + dz, 4) * 2 + lax.rem(self.c + dc, 2)

    def in_narrow(self, dy, dh):
        return lax.rem(self.y + dy, 4) * 2 + lax.rem(self.zh + dh, 2)

    def wide_peer(self, dx, dz, dc):
        return {"wide": self.in_wide(dx, dz, dc), "narrow": self.narrow}

    def narrow_peer(self, dy, dh):
        return {"wide": self.wide, "narrow": self.in_narrow(dy, dh)}


def greet(peers):
    barrier = pltpu.get_barrier_semaphore()
    for peer in peers:
        pl.semaphore_signal(barrier, inc=1, device_id=peer, device_id_type=MESH)
    pl.semaphore_wait(barrier, len(peers))


def send(src, dst, send_sem, recv_sem, peer):
    copy = pltpu.make_async_remote_copy(
        src_ref=src,
        dst_ref=dst,
        send_sem=send_sem,
        recv_sem=recv_sem,
        device_id=peer,
        device_id_type=MESH,
    )
    copy.start()
    return copy


def arrived(dst, sem, peer):
    pltpu.make_async_remote_copy(
        src_ref=dst, dst_ref=dst, send_sem=sem, recv_sem=sem, device_id=peer, device_id_type=MESH
    ).wait_recv()


WIDE_HOPS = [(1, 0, 0), (2, 0, 0), (3, 0, 0), (0, 1, 0), (0, 2, 0), (0, 3, 0), (0, 0, 1)]


def slot(a, k, c):
    return (a % 4) * 8 + (k % 4) * 2 + c % 2


def project_kernel(
    hidden_ref,
    gain_ref,
    shift_ref,
    w_qkv_ref,
    w_up_ref,
    qkv_bias_ref,
    up_bias_ref,
    cos_ref,
    sin_lo_ref,
    sin_hi_ref,
    out_q,
    out_u1,
    out_u2,
    gathered,
    stats,
    stats_part,
    normed,
    part_q,
    part_u1,
    part_u2,
    *rest,
):
    n_ch = 3
    outs = [out_q, out_u1, out_u2]
    parts = [part_q, part_u1, part_u2]
    mids = [rest[4 * i : 4 * i + 4] for i in range(n_ch)]
    rest = rest[4 * n_ch :]
    wide_send, wide_recv, stat_send, stat_recv, sn_send, sn_recv, ch_send, ch_recv = rest
    me = Place()
    rows = 64
    greet(
        [me.wide_peer(*hop) for hop in WIDE_HOPS]
        + [me.narrow_peer(dy, dh) for dy in range(4) for dh in range(2) if dy or dh]
    )
    open_copies = []
    counts = {"wide": 0, "stat": 0}

    def push(kind, block, rel, hop, own):
        buf, ss, rs = (
            (gathered, wide_send, wide_recv) if kind == "wide" else (stats, stat_send, stat_recv)
        )
        i = counts[kind]
        counts[kind] = i + 1
        index = me.in_wide(*rel)
        src = hidden_ref if own and kind == "wide" else buf.at[index]
        there = slot(rel[0] - hop[0], rel[1] - hop[1], rel[2] - hop[2])
        open_copies.append(
            send(src, buf.at[index], ss.at[i], rs.at[there], me.wide_peer(*hop))
        )

    def wait_block(kind, rel):
        buf, rs = (gathered, wide_recv) if kind == "wide" else (stats, stat_recv)
        arrived(buf.at[me.in_wide(*rel)], rs.at[slot(*rel)], me.wide_peer(0, 0, 1))

    def normalise(block, index):
        as_float = block.astype(F32)
        line = stats[index][0:1, :]
        lane = lax.broadcasted_iota(jnp.int32, (rows, 128), 1)
        row = lax.broadcasted_iota(jnp.int32, (rows, 128), 0)
        average = jnp.sum(jnp.where(lane == row, line, 0.0), axis=1, keepdims=True)
        inverse = jnp.sum(jnp.where(lane == row + rows, line, 0.0), axis=1, keepdims=True)
        scaled = (as_float - average) * inverse
        for i in range(2):
            normed[i, index] = (scaled * gain_ref[i : i + 1, :] + shift_ref[i : i + 1, :]).astype(BF16)

    for hop in WIDE_HOPS:
        push("wide", None, (0, 0, 0), hop, True)

    as_float = hidden_ref[...].astype(F32)
    ones = jnp.ones((8, as_float.shape[1]), F32)

    def row_sums(v):
        return lax.dot_general(
            ones, v, (((1,), (1,)), ((), ())), precision=lax.Precision.HIGHEST,
            preferred_element_type=F32,
        )

    stats_part[me.narrow] = jnp.concatenate([row_sums(as_float), row_sums(as_float * as_float)], axis=1)
    i = 0
    for dy in range(4):
        for dh in range(2):
            if dy or dh:
                there = ((-dy) % 4) * 2 + (-dh) % 2
                open_copies.append(
                    send(
                        stats_part.at[me.narrow], stats_part.at[me.narrow],
                        sn_send.at[i], sn_recv.at[there], me.narrow_peer(dy, dh),
                    )
                )
                i += 1
    for dy in range(4):
        for dh in range(2):
            if dy or dh:
                arrived(
                    stats_part.at[me.in_narrow(dy, dh)], sn_recv.at[dy * 2 + dh], me.narrow_peer(dy, dh)
                )
    total = stats_part[0]
    for i in range(1, 8):
        total = total + stats_part[i]
    average = total[:, :rows] / D
    variance = total[:, rows:] / D - average * average
    stats[me.wide] = jnp.concatenate([average, lax.rsqrt(variance + 1e-05)], axis=1)
    for hop in WIDE_HOPS:
        push("stat", None, (0, 0, 0), hop, True)
    normalise(hidden_ref[...], me.wide)

    x_hops = [(1, 0, 0), (3, 0, 0), (2, 0, 0)]
    core = (0, 0, 1)
    ready = []
    for k in (1, 3, 2):
        rel = (0, k, 0)
        for kind in ("stat", "wide"):
            wait_block(kind, rel)
            for hop in x_hops:
                push(kind, None, rel, hop, False)
            push(kind, None, rel, core, False)
        normalise(gathered[me.in_wide(*rel)], me.in_wide(*rel))
    for k in (0, 1, 3, 2):
        for a in (1, 3, 2):
            rel = (a, k, 0)
            for kind in ("stat", "wide"):
                wait_block(kind, rel)
                push(kind, None, rel, core, False)
            normalise(gathered[me.in_wide(*rel)], me.in_wide(*rel))
    for k in (0, 1, 3, 2):
        for a in (0, 1, 3, 2):
            rel = (a, k, 1)
            for kind in ("stat", "wide"):
                wait_block(kind, rel)
            normalise(gathered[me.in_wide(*rel)], me.in_wide(*rel))

    def rows_of(which, owner):
        return normed[which, pl.ds(owner * 4, 4)].reshape(256, normed.shape[-1])

    @pl.loop(0, 8)
    def _(owner):
        part_q[owner] = jnp.dot(rows_of(0, owner), w_qkv_ref[...], preferred_element_type=F32).astype(BF16)

    n_sent = [0] * n_ch
    up, down = me.narrow_peer(1, 0), me.narrow_peer(3, 0)
    across = me.narrow_peer(0, 1)
    ra, rb = pl.ds(0, 128), pl.ds(128, 128)

    def put(ch, src, dst, sem, peer):
        i = n_sent[ch]
        n_sent[ch] = i + 1
        open_copies.append(send(src, dst, ch_send.at[ch, i], ch_recv.at[ch, sem], peer))

    def got(ch, dst, sem):
        arrived(dst, ch_recv.at[ch, sem], up)

    def scatter_first(ch, h):
        part, (first, side, _, _) = parts[ch], mids[ch]
        far, nxt, prv = me.in_narrow(2, h), me.in_narrow(1, h), me.in_narrow(3, h)
        put(ch, part.at[far, ra], first.at[h, 0], 6 * h + 0, up)
        put(ch, part.at[far, rb], first.at[h, 1], 6 * h + 1, down)
        put(ch, part.at[nxt, rb], side.at[h, 0, rb], 6 * h + 2, up)
        put(ch, part.at[prv, ra], side.at[h, 1, ra], 6 * h + 3, down)

    def scatter_second(ch, h):
        part, (first, side, _, _) = parts[ch], mids[ch]
        nxt, prv = me.in_narrow(1, h), me.in_narrow(3, h)
        got(ch, first.at[h, 0], 6 * h + 0)
        part[nxt, ra] = (part[nxt, ra].astype(F32) + first[h, 0].astype(F32)).astype(BF16)
        put(ch, part.at[nxt, ra], side.at[h, 0, ra], 6 * h + 4, up)
        got(ch, first.at[h, 1], 6 * h + 1)
        part[prv, rb] = (part[prv, rb].astype(F32) + first[h, 1].astype(F32)).astype(BF16)
        put(ch, part.at[prv, rb], side.at[h, 1, rb], 6 * h + 5, down)

    def sum_of(ch, h):
        part, (first, side, _, _) = parts[ch], mids[ch]
        got(ch, side.at[h, 0, rb], 6 * h + 2)
        got(ch, side.at[h, 1, ra], 6 * h + 3)
        got(ch, side.at[h, 0, ra], 6 * h + 4)
        got(ch, side.at[h, 1, rb], 6 * h + 5)
        own = me.in_narrow(0, h)
        return part[own].astype(F32) + side[h, 0].astype(F32) + side[h, 1].astype(F32)

    def scatter_across(ch):
        zbuf = mids[ch][2]
        zbuf[0] = sum_of(ch, 1).astype(BF16)
        put(ch, zbuf.at[0], zbuf.at[1], 12, across)

    def finish(ch):
        zbuf = mids[ch][2]
        summed = sum_of(ch, 0)
        got(ch, zbuf.at[1], 12)
        summed = summed + zbuf[1].astype(F32)
        if ch == 0:
            u = summed + qkv_bias_ref[...]
            u = (
                u * cos_ref[...]
                + pltpu.roll(u, QKV_PAD - ROTARY // 2, 1) * sin_lo_ref[...]
                + pltpu.roll(u, ROTARY // 2, 1) * sin_hi_ref[...]
            )
        else:
            u = summed + up_bias_ref[ch - 1 : ch, :]
            u = 0.5 * u * (1.0 + lax.erf(u * (0.5**0.5)))
        out = outs[ch]
        out[me.narrow] = u.astype(BF16)
        mine = out.at[me.narrow]
        put(ch, mine, mine, 13, across)
        put(ch, mine, mine, 14, up)
        put(ch, mine, mine, 15, down)

    def relay_half(ch, h):
        out = outs[ch]
        below, above = me.in_narrow(3, h), me.in_narrow(1, h)
        got(ch, out.at[below], 14 + 4 * h)
        put(ch, out.at[below, ra], out.at[below, ra], 16 + 4 * h, up)
        got(ch, out.at[above], 15 + 4 * h)
        put(ch, out.at[above, rb], out.at[above, rb], 17 + 4 * h, down)

    def relay_across(ch):
        block = outs[ch].at[me.in_narrow(0, 1)]
        got(ch, block, 13)
        put(ch, block, block, 18, up)
        put(ch, block, block, 19, down)

    def gather_last(ch):
        for h in range(2):
            far = outs[ch].at[me.in_narrow(2, h)]
            got(ch, far.at[ra], 16 + 4 * h)
            got(ch, far.at[rb], 17 + 4 * h)

    scatter_first(0, 1)
    scatter_first(0, 0)

    @pl.loop(0, 8)
    def _(owner):
        up_part = jnp.dot(rows_of(1, owner), w_up_ref[...], preferred_element_type=F32).astype(BF16)
        part_u1[owner] = up_part[:, :HALF_FF]
        part_u2[owner] = up_part[:, HALF_FF:]

    scatter_second(0, 1)
    scatter_second(0, 0)
    scatter_first(1, 1)
    scatter_first(1, 0)
    scatter_across(0)
    scatter_second(1, 1)
    scatter_second(1, 0)
    scatter_first(2, 1)
    scatter_first(2, 0)
    finish(0)
    scatter_across(1)
    scatter_second(2, 1)
    scatter_second(2, 0)
    relay_half(0, 0)
    relay_across(0)
    finish(1)
    scatter_across(2)
    relay_half(0, 1)
    relay_half(1, 0)
    relay_across(1)
    finish(2)
    relay_half(1, 1)
    relay_half(2, 0)
    relay_across(2)
    relay_half(2, 1)
    for ch in range(n_ch):
        gather_last(ch)
    for copy in open_copies:
        copy.wait_send()


def project(hidden, gain, shift, w_qkv, w_up, qkv_bias, up_bias, cos, sin_lo, sin_hi):
    width = hidden.shape[1]
    cols = [QKV_PAD, HALF_FF, HALF_FF]
    mids = []
    for c in cols:
        mids += [VM((2, 2, 128, c), BF16), VM((2, 2, 256, c), BF16), VM((2, 256, c), BF16), VM((8, 128), F32)]
    return pl.pallas_call(
        project_kernel,
        out_shape=[jax.ShapeDtypeStruct((8, 256, c), BF16) for c in cols],
        in_specs=[pl.BlockSpec(memory_space=VM)] * 10,
        out_specs=[pl.BlockSpec(memory_space=VM)] * 3,
        scratch_shapes=[
            VM((32, 64, width), BF16),
            VM((32, 8, 128), F32),
            VM((8, 8, 128), F32),
            VM((2, 32, 64, width), BF16),
        ]
        + [VM((8, 256, c), BF16) for c in cols]
        + mids
        + [DMA((31,)), DMA((32,)), DMA((31,)), DMA((32,)), DMA((7,)), DMA((8,)), DMA((3, 22)), DMA((3, 22))],
        compiler_params=pltpu.CompilerParams(
            collective_id=0, has_side_effects=True, vmem_limit_bytes=56 << 20
        ),
        name="project",
    )(hidden, gain, shift, w_qkv, w_up, qkv_bias, up_bias, cos, sin_lo, sin_hi)


def attend_kernel(lens, sinks, pages, qkv_ref, out_ref, cache_ref):
    block = pl.program_id(0)
    queries, span, tail = 256, 384, 128
    total = qkv_ref.shape[0]
    first = block * queries
    width = out_ref.shape[1]

    def of_sequence(token):
        end = 0
        start = jnp.zeros_like(token)
        sink = jnp.zeros_like(token) + sinks[0]
        for s in range(8):
            end = end + lens[s]
            after = token >= end
            start = jnp.where(after, end, start)
            if s < 7:
                sink = jnp.where(after, sinks[s + 1], sink)
        return start, start + sink

    query = first + lax.broadcasted_iota(jnp.int32, (queries, 1), 0)
    start, sink_end = of_sequence(query)
    near = pl.multiple_of(jnp.maximum(first - WINDOW, 0), WINDOW)
    head_start, _ = of_sequence(first)
    far = pl.multiple_of(jnp.minimum(head_start // 16 * 16, total - tail), 16)
    near_key = near + lax.broadcasted_iota(jnp.int32, (1, span), 1)
    far_key = far + lax.broadcasted_iota(jnp.int32, (1, tail), 1)

    def allowed(key):
        return (key >= start) & (key <= query) & ((query - key < WINDOW) | (key < sink_end))

    near_ok = allowed(near_key)
    far_ok = allowed(far_key) & (far_key < near)
    mask = jnp.concatenate([near_ok, far_ok], axis=1)
    q = qkv_ref[pl.ds(first, queries), :][:, :width]
    near_rows = qkv_ref[pl.ds(near, span), :]
    far_rows = qkv_ref[pl.ds(far, tail), :]
    keys = jnp.concatenate([near_rows[:, width : 2 * width], far_rows[:, width : 2 * width]], axis=0)
    values = jnp.concatenate(
        [near_rows[:, 2 * width : 3 * width], far_rows[:, 2 * width : 3 * width]], axis=0
    )
    lane = lax.broadcasted_iota(jnp.int32, (queries, width), 1)
    result = None
    for head in range(width // HEAD_DIM):
        in_head = (lane >= head * HEAD_DIM) & (lane < (head + 1) * HEAD_DIM)
        masked_q = jnp.where(in_head, q, jnp.zeros_like(q))
        scores = lax.dot_general(
            masked_q, keys, (((1,), (1,)), ((), ())), preferred_element_type=F32
        ) * (1.0 / HEAD_DIM**0.5)
        scores = jnp.where(mask, scores, F32(-1e30))
        weights = jnp.exp(scores - jnp.max(scores, axis=1, keepdims=True))
        probs = (weights / jnp.sum(weights, axis=1, keepdims=True)).astype(BF16)
        got = jnp.dot(probs, values, preferred_element_type=F32)
        result = got if result is None else jnp.where(in_head, got, result)
    out_ref[...] = result.astype(BF16)
    for j in range(2):
        row = pl.multiple_of(pages[block * 2 + j] * PAGE, PAGE)
        page = qkv_ref[pl.ds(row, PAGE), :]
        cache_ref[0, j] = page[:, width : 2 * width]
        cache_ref[1, j] = page[:, 2 * width : 3 * width]


def attend(lens, sinks, pages, qkv, width):
    return pl.pallas_call(
        attend_kernel,
        out_shape=[
            jax.ShapeDtypeStruct((qkv.shape[0], width), BF16),
            jax.ShapeDtypeStruct((2, 16, PAGE, width), BF16),
        ],
        grid_spec=pltpu.PrefetchScalarGridSpec(
            num_scalar_prefetch=3,
            grid=(8,),
            in_specs=[pl.BlockSpec(qkv.shape, lambda b, *_: (0, 0))],
            out_specs=[
                pl.BlockSpec((256, width), lambda b, *_: (b, 0)),
                pl.BlockSpec((2, 2, PAGE, width), lambda b, *_: (0, b, 0, 0)),
            ],
        ),
        name="attend",
    )(lens, sinks, pages, qkv)


def output_kernel(
    att_ref,
    u1_ref,
    u2_ref,
    w_out_ref,
    w_down_ref,
    hidden_ref,
    bias_ref,
    out_ref,
    products,
    core_in,
    halves,
    x_in,
    z_out,
    z_in,
    core_send,
    core_recv,
    x_send,
    x_recv,
    z_send,
    z_recv,
):
    me = Place()
    greet([me.wide_peer(*hop) for hop in WIDE_HOPS])
    open_copies = []
    sibling = me.wide_peer(0, 0, 1)
    width = out_ref.shape[1]
    order = (2, 1, 3, 0)
    for half in range(2):
        for dx in order:
            n = lax.rem(me.x + dx, 4) * 2 + half
            o = jnp.dot(u1_ref[n], w_down_ref[:HALF_FF, :], preferred_element_type=F32)
            o = o + jnp.dot(u2_ref[n], w_down_ref[HALF_FF:, :], preferred_element_type=F32)
            o = o + jnp.dot(att_ref[n], w_out_ref[...], preferred_element_type=F32)
            products[n] = o.astype(BF16).reshape(2, 2, 64, width)
            for j in range(2):
                i = half * 8 + dx * 2 + j
                open_copies.append(
                    send(
                        products.at[n, j, 1 - me.c], core_in.at[n, j], core_send.at[i], core_recv.at[i], sibling
                    )
                )
    for half in range(2):
        for dx in order:
            n = lax.rem(me.x + dx, 4) * 2 + half
            for j in range(2):
                arrived(core_in.at[n, j], core_recv.at[half * 8 + dx * 2 + j], sibling)
            halves[half, dx] = (products[n, :, me.c].astype(F32) + core_in[n].astype(F32)).astype(BF16)
            if dx:
                i = half * 3 + dx - 1
                there = half * 3 + (4 - dx) - 1
                open_copies.append(
                    send(
                        halves.at[half, dx], x_in.at[half, 3 - dx],
                        x_send.at[i], x_recv.at[there], me.wide_peer(dx, 0, 0),
                    )
                )
    for half in range(2):
        total = halves[half, 0].astype(F32)
        for dx in (1, 3, 2):
            arrived(x_in.at[half, dx - 1], x_recv.at[half * 3 + dx - 1], sibling)
            total = total + x_in[half, dx - 1].astype(F32)
        z_out[half] = total.astype(BF16)
        for j in range(2):
            to = half * 2 + j
            peer = {"wide": me.x * 8 + to * 2 + me.c, "narrow": me.narrow}

            @pl.when(me.zl != to)
            def _():
                send(z_out.at[half, j], z_in.at[me.zl], z_send.at[to], z_recv.at[me.zl], peer)

    total = z_out[me.zl // 2, me.zl % 2].astype(F32) + hidden_ref[...].astype(F32) + bias_ref[...]
    for k in range(1, 4):
        source = lax.rem(me.zl + k, 4)
        arrived(z_in.at[source], z_recv.at[source], sibling)
        total = total + z_in[source].astype(F32)
    out_ref[...] = total.astype(BF16)
    for copy in open_copies:
        copy.wait_send()
    for k in range(1, 4):
        to = lax.rem(me.zl + k, 4)
        pltpu.make_async_remote_copy(
            src_ref=z_out.at[to // 2, to % 2], dst_ref=z_in.at[me.zl], send_sem=z_send.at[to],
            recv_sem=z_recv.at[me.zl], device_id=me.wide_peer(0, k, 0), device_id_type=MESH,
        ).wait_send()


def output(att, u1, u2, w_out, w_down, hidden, bias):
    width = hidden.shape[1]
    return pl.pallas_call(
        output_kernel,
        out_shape=jax.ShapeDtypeStruct(hidden.shape, BF16),
        in_specs=[pl.BlockSpec(memory_space=VM)] * 7,
        out_specs=pl.BlockSpec(memory_space=VM),
        scratch_shapes=[
            VM((8, 2, 2, 64, width), BF16),
            VM((8, 2, 64, width), BF16),
            VM((2, 4, 2, 64, width), BF16),
            VM((2, 3, 2, 64, width), BF16),
            VM((2, 2, 64, width), BF16),
            VM((4, 64, width), BF16),
            DMA((16,)),
            DMA((16,)),
            DMA((6,)),
            DMA((6,)),
            DMA((4,)),
            DMA((4,)),
        ],
        compiler_params=pltpu.CompilerParams(
            collective_id=1, has_side_effects=True, vmem_limit_bytes=56 << 20
        ),
        name="output",
    )(att, u1, u2, w_out, w_down, hidden, bias)


def rotation_tables(narrow_index, seq_lens):
    token = narrow_index * 256 + jnp.arange(256, dtype=jnp.int32)
    ends = jnp.cumsum(seq_lens)
    after = token[:, None] >= ends[None, :]
    position = token - jnp.sum(jnp.where(after, seq_lens[None, :], 0), axis=1)
    half = ROTARY // 2
    freq_index = jnp.arange(half, dtype=F32)
    inverse = jnp.power(F32(10000.0), -2.0 * freq_index / ROTARY)
    angles = position.astype(F32)[:, None] * inverse[None, :]
    cosine, sine = jnp.cos(angles), jnp.sin(angles)

    def spread(parts, rest):
        head = jnp.concatenate(parts + [jnp.full((256, HEAD_DIM - ROTARY), rest, F32)], axis=1)
        return jnp.concatenate(
            [jnp.tile(head, (1, 4)), jnp.full((256, QKV_PAD - 4 * HEAD_DIM), rest, F32)], axis=1
        )

    none = jnp.zeros_like(sine)
    return spread([cosine, cosine], 1.0), spread([-sine, none], 0.0), spread([none, sine], 0.0)


def local(
    hidden_in,
    w_query,
    w_key,
    w_value,
    qkv_bias,
    w_up,
    up_bias,
    w_attn_out,
    w_down,
    out_bias,
    norm_gain,
    norm_bias,
    seq_lens,
    sink_count,
    page_table,
):
    narrow_index = lax.axis_index("narrow")
    feat, head_cols = w_query.shape
    pad = QKV_PAD - 3 * head_cols
    w_qkv = jnp.concatenate([w_query, w_key, w_value, jnp.zeros((feat, pad), BF16)], axis=1)
    bias = jnp.concatenate([qkv_bias.reshape(1, -1), jnp.zeros((1, pad), F32)], axis=1)
    cos, sin_lo, sin_hi = rotation_tables(narrow_index, seq_lens)
    qkv, u1, u2 = project(
        hidden_in, norm_gain, norm_bias, w_qkv, w_up, bias, up_bias.reshape(2, HALF_FF), cos, sin_lo, sin_hi
    )
    pages_local = page_table.shape[0] // 8
    slot_ids = narrow_index * pages_local + jnp.arange(pages_local, dtype=jnp.int32)
    matches = (page_table[None, :] == slot_ids[:, None]).astype(jnp.int32)
    source_page = jnp.sum(
        matches * jnp.arange(page_table.shape[0], dtype=jnp.int32)[None, :], axis=1
    )
    attended, cache = attend(seq_lens, sink_count, source_page, qkv.reshape(2048, QKV_PAD), head_cols)
    hidden_out = output(
        attended.reshape(8, 256, head_cols), u1, u2, w_attn_out, w_down, hidden_in, out_bias.reshape(1, -1)
    )
    return (hidden_out, cache)


def solution(mesh):
    in_specs = (
        P("wide", "narrow"),
        P("narrow", "wide"),
        P("narrow", "wide"),
        P("narrow", "wide"),
        P(None, "wide"),
        P("narrow", "wide"),
        P("wide"),
        P("wide", "narrow"),
        P("wide", "narrow"),
        P("narrow"),
        P(None, "narrow"),
        P(None, "narrow"),
        P(),
        P(),
        P(),
    )
    out_specs = (P("wide", "narrow"), P(None, "narrow", None, "wide"))
    return jax.shard_map(local, mesh=mesh, in_specs=in_specs, out_specs=out_specs, check_vma=False)
```

```python
import jax
import jax.numpy as jnp
import numpy as np
from jax import lax
from jax.experimental import pallas as pl
from jax.experimental.pallas import tpu as pltpu
from jax.sharding import PartitionSpec as P

D = 6144
HEAD_DIM = 96
ROTARY = 24
PAGE = 16
WINDOW = 128
SEQS = 8
NPAGES = 128
TOKENS = 2048
MESH = pl.DeviceIdType.MESH
F32 = jnp.float32
BF16 = jnp.bfloat16
VM = pltpu.VMEM
DMA = pltpu.SemaphoreType.DMA
FEAT = 768
HEADS2 = 192
ROT_COLS = 2 * HEADS2
QKV_PAD = 640
UNITS = 768
BLOCK = 64
OWN = 128
COLS = {"q": QKV_PAD, "u": UNITS}


class Place:
    def __init__(self):
        wide = lax.axis_index("wide")
        narrow = lax.axis_index("narrow")
        self.x, self.zl, self.c = wide // 8, (wide // 2) % 4, wide % 2
        self.y, self.zh = narrow // 2, narrow % 2
        self.wide, self.narrow = wide, narrow

    def in_wide(self, dx, dz, dc):
        return lax.rem(self.x + dx, 4) * 8 + lax.rem(self.zl + dz, 4) * 2 + lax.rem(self.c + dc, 2)

    def in_narrow(self, dy, dh):
        return lax.rem(self.y + dy, 4) * 2 + lax.rem(self.zh + dh, 2)

    def wide_peer(self, dx, dz, dc):
        return {"wide": self.in_wide(dx, dz, dc), "narrow": self.narrow}

    def narrow_peer(self, dy, dh):
        return {"wide": self.wide, "narrow": self.in_narrow(dy, dh)}


def greet(peers):
    barrier = pltpu.get_barrier_semaphore()
    for peer in peers:
        pl.semaphore_signal(barrier, inc=1, device_id=peer, device_id_type=MESH)
    pl.semaphore_wait(barrier, len(peers))


def send(src, dst, send_sem, recv_sem, peer):
    copy = pltpu.make_async_remote_copy(
        src_ref=src,
        dst_ref=dst,
        send_sem=send_sem,
        recv_sem=recv_sem,
        device_id=peer,
        device_id_type=MESH,
    )
    copy.start()
    return copy


def arrived(dst, sem, peer):
    pltpu.make_async_remote_copy(
        src_ref=dst, dst_ref=dst, send_sem=sem, recv_sem=sem, device_id=peer, device_id_type=MESH
    ).wait_recv()


WIDE_HOPS = [(0, 2, 0), (1, 0, 0), (3, 0, 0), (2, 0, 0), (0, 1, 0), (0, 3, 0), (0, 0, 1)]
NARROW_HOPS = [(dy, dh) for dy in range(4) for dh in range(2) if dy or dh]
KINDS = ("q", "u")


def slot(a, k, c):
    return (a % 4) * 8 + (k % 4) * 2 + c % 2


def project_kernel(
    lens,
    hidden_ref,
    gain_ref,
    shift_ref,
    w_query,
    w_key,
    w_value,
    w_up,
    qkv_bias_ref,
    up_bias_ref,
    qkv,
    units,
    w_qkv,
    gathered,
    stats,
    stats_part,
    tables,
    normed,
    part_q0,
    part_q1,
    part_u0,
    part_u1,
    first_q0,
    first_q1,
    first_u0,
    first_u1,
    side_q0,
    side_q1,
    side_u0,
    side_u1,
    across_q0,
    across_q1,
    across_u0,
    across_u1,
    wide_send,
    wide_recv,
    stat_send,
    stat_recv,
    sn_send,
    sn_recv,
    unit_send,
    unit_recv,
):
    parts = {"q": (part_q0, part_q1), "u": (part_u0, part_u1)}
    firsts = {"q": (first_q0, first_q1), "u": (first_u0, first_u1)}
    sides = {"q": (side_q0, side_q1), "u": (side_u0, side_u1)}
    acrosses = {"q": (across_q0, across_q1), "u": (across_u0, across_u1)}
    me = Place()
    parity = me.zl % 2
    sibling = me.wide_peer(0, 0, 1)
    greet([me.wide_peer(*hop) for hop in WIDE_HOPS] + [me.narrow_peer(*hop) for hop in NARROW_HOPS])
    open_copies = []

    counts = {"wide": 0, "stat": 0}

    def push(kind, rel, hop, own=False):
        buf, ss, rs = (
            (gathered, wide_send, wide_recv) if kind == "wide" else (stats, stat_send, stat_recv)
        )
        i = counts[kind]
        counts[kind] = i + 1
        index = me.in_wide(*rel)
        src = hidden_ref if own and kind == "wide" else buf.at[index]
        there = slot(rel[0] - hop[0], rel[1] - hop[1], rel[2] - hop[2])
        open_copies.append(send(src, buf.at[index], ss.at[i], rs.at[there], me.wide_peer(*hop)))

    def wait_block(kind, rel):
        buf, rs = (gathered, wide_recv) if kind == "wide" else (stats, stat_recv)
        arrived(buf.at[me.in_wide(*rel)], rs.at[slot(*rel)], sibling)

    def normalise(block, rel):
        index = me.in_wide(*rel)
        as_float = block.astype(F32)
        line = stats[index][0:1, :]
        lane = lax.broadcasted_iota(jnp.int32, (BLOCK, 128), 1)
        row = lax.broadcasted_iota(jnp.int32, (BLOCK, 128), 0)
        average = jnp.sum(jnp.where(lane == row, line, 0.0), axis=1, keepdims=True)
        inverse = jnp.sum(jnp.where(lane == row + BLOCK, line, 0.0), axis=1, keepdims=True)
        scaled = (as_float - average) * inverse
        owner = lax.rem(me.x + rel[0], 4) * 2 + lax.rem(me.zl + rel[1], 4) // 2
        core = lax.rem(me.c + rel[2], 2)
        for i in range(2):
            normed[i, rel[1] % 2, owner, core] = (
                scaled * gain_ref[i : i + 1, :] + shift_ref[i : i + 1, :]
            ).astype(BF16)

    own, core_hop = (0, 0, 0), (0, 0, 1)
    x_hops = [(1, 0, 0), (3, 0, 0), (2, 0, 0)]
    for hop in [(0, 2, 0)] + x_hops + [core_hop]:
        push("wide", own, hop, True)
    lanes = lax.broadcasted_iota(jnp.int32, (BLOCK, 128), 1)
    rows = lax.broadcasted_iota(jnp.int32, (BLOCK, 128), 0)
    as_float = hidden_ref[...].astype(F32)
    sums = jnp.sum(as_float, axis=1, keepdims=True)
    squares = jnp.sum(as_float * as_float, axis=1, keepdims=True)
    line = jnp.where(lanes == rows, sums, 0.0) + jnp.where(lanes == rows + BLOCK, squares, 0.0)
    stats_part[me.narrow] = jnp.broadcast_to(jnp.sum(line, axis=0, keepdims=True), (8, 128))
    for i, (dy, dh) in enumerate(NARROW_HOPS):
        mine = stats_part.at[me.narrow]
        there = ((-dy) % 4) * 2 + (-dh) % 2
        open_copies.append(send(mine, mine, sn_send.at[i], sn_recv.at[there], me.narrow_peer(dy, dh)))
    for hop in [(0, 1, 0), (0, 3, 0)]:
        push("wide", own, hop, True)
    rel = (0, 2, 0)
    wait_block("wide", rel)
    for hop in x_hops + [core_hop]:
        push("wide", rel, hop)
    for dy, dh in NARROW_HOPS:
        arrived(stats_part.at[me.in_narrow(dy, dh)], sn_recv.at[dy * 2 + dh], sibling)
    total = stats_part[0]
    for i in range(1, 8):
        total = total + stats_part[i]
    average = total[:, :BLOCK] / D
    variance = total[:, BLOCK:] / D - average * average
    stats[me.wide] = jnp.concatenate([average, lax.rsqrt(variance + 1e-05)], axis=1)
    for hop in WIDE_HOPS:
        push("stat", own, hop, True)
    normalise(hidden_ref[...], own)
    wait_block("stat", rel)
    for hop in x_hops + [core_hop]:
        push("stat", rel, hop)
    normalise(gathered[me.in_wide(*rel)], rel)

    pad = QKV_PAD - 3 * HEADS2
    qkv_bias = jnp.concatenate(
        [qkv_bias_ref[i : i + 1, :] for i in range(3)] + [jnp.zeros((1, pad), F32)], axis=1
    )
    up_bias = up_bias_ref[...].reshape(1, UNITS)
    w_qkv[...] = jnp.concatenate(
        [w_query[...], w_key[...], w_value[...], jnp.zeros((pad, FEAT), BF16)], axis=0
    ).T

    def sequence_start(token):
        end = 0
        start = token * 0
        for s in range(SEQS):
            end = end + lens[s]
            start = jnp.where(token >= end, end, start)
        return start

    def side_of(t):
        return parity if t == 0 else 1 - parity

    def first_token(t, owner):
        return owner * (2 * OWN) + side_of(t) * OWN

    def rotation_factors():
        lane = lax.broadcasted_iota(jnp.int32, (1, ROT_COLS), 1) % HEAD_DIM
        step = lane % (ROTARY // 2)
        inverses = np.power(np.float32(10000.0), (-2.0 * np.arange(12) / ROTARY).astype(np.float32))
        frequency = jnp.zeros((1, ROT_COLS), F32)
        for i in range(ROTARY // 2):
            frequency = jnp.where(step == i, F32(inverses[i]), frequency)
        for t in range(2):
            token = first_token(t, me.narrow) + lax.broadcasted_iota(jnp.int32, (OWN, 1), 0)
            position = (token - sequence_start(token)).astype(F32)
            angle = jnp.where(lane < ROTARY, position * frequency, 0.0)
            sine = jnp.sin(angle)
            tables[t, 0] = jnp.cos(angle)
            tables[t, 1] = jnp.where(lane < ROTARY // 2, -sine, 0.0)
            tables[t, 2] = jnp.where(lane < ROTARY // 2, 0.0, sine)

    def from_x(k, a):
        rel = (a, k, 0)
        for kind in ("wide", "stat"):
            wait_block(kind, rel)
            push(kind, rel, core_hop)
        normalise(gathered[me.in_wide(*rel)], rel)

    def from_sibling(ks):
        for k in ks:
            for a in (0, 1, 3, 2):
                rel = (a, k, 1)
                for kind in ("wide", "stat"):
                    wait_block(kind, rel)
                normalise(gathered[me.in_wide(*rel)], rel)

    def gather_first():
        for a in (1, 3, 2):
            from_x(0, a)
        for k in (1, 3):
            rel = (0, k, 0)
            wait_block("stat", rel)
            for hop in x_hops + [core_hop]:
                push("stat", rel, hop)
            wait_block("wide", rel)
            push("wide", rel, core_hop)
        for a in (1, 3):
            from_x(2, a)
        for k in (1, 3):
            for hop in x_hops:
                push("wide", (0, k, 0), hop)
        from_x(2, 2)
        from_sibling((0, 2))

    def gather_second():
        for k in (1, 3):
            normalise(gathered[me.in_wide(0, k, 0)], (0, k, 0))
        for k in (1, 3):
            for a in (1, 3, 2):
                from_x(k, a)
        from_sibling((1, 3))

    def multiply(kind, t):
        which, weight = (0, w_qkv) if kind == "q" else (1, w_up)
        part = parts[kind][t]

        @pl.loop(0, 4)
        def _(pair):
            rows = normed[which, t, pl.ds(pair * 2, 2)].reshape(2 * OWN, FEAT)
            product = jnp.dot(rows, weight[...], preferred_element_type=F32).astype(BF16)
            part[pl.ds(pair * 2, 2)] = product.reshape(2, OWN, COLS[kind])

    sent = {}
    up, down, across = me.narrow_peer(1, 0), me.narrow_peer(3, 0), me.narrow_peer(0, 1)
    whole, ra, rb = (0, OWN), (0, OWN // 2), (OWN // 2, OWN // 2)

    def number(u):
        return KINDS.index(u[0]) * 2 + u[1]

    def put(u, src, dst, sem, peer):
        i = sent.get(u, 0)
        sent[u] = i + 1
        n = number(u)
        open_copies.append(send(src, dst, unit_send.at[n, i], unit_recv.at[n, sem], peer))

    def got(u, dst, sem):
        arrived(dst, unit_recv.at[number(u), sem], up)

    def bufs(u):
        kind, t = u
        return parts[kind][t], firsts[kind][t], sides[kind][t], acrosses[kind][t]

    def result(u, owner, rows):
        kind, t = u
        if kind == "q":
            return qkv.at[owner * 2 + side_of(t), pl.ds(*rows)]
        return units.at[owner * 2 + side_of(t), pl.ds(*rows)]

    def scatter_first(u):
        part, first, side, _ = bufs(u)
        for h in (1, 0):
            far, nxt, prv = me.in_narrow(2, h), me.in_narrow(1, h), me.in_narrow(3, h)
            a, b = pl.ds(*ra), pl.ds(*rb)
            put(u, part.at[far, a], first.at[h, 0], 6 * h + 0, up)
            put(u, part.at[far, b], first.at[h, 1], 6 * h + 1, down)
            put(u, part.at[nxt, b], side.at[h, 0, b], 6 * h + 2, up)
            put(u, part.at[prv, a], side.at[h, 1, a], 6 * h + 3, down)

    def scatter_second(u):
        part, first, side, _ = bufs(u)
        a, b = pl.ds(*ra), pl.ds(*rb)
        for h in (1, 0):
            nxt, prv = me.in_narrow(1, h), me.in_narrow(3, h)
            got(u, first.at[h, 0], 6 * h + 0)
            part[nxt, a] = (part[nxt, a].astype(F32) + first[h, 0].astype(F32)).astype(BF16)
            put(u, part.at[nxt, a], side.at[h, 0, a], 6 * h + 4, up)
            got(u, first.at[h, 1], 6 * h + 1)
            part[prv, b] = (part[prv, b].astype(F32) + first[h, 1].astype(F32)).astype(BF16)
            put(u, part.at[prv, b], side.at[h, 1, b], 6 * h + 5, down)

    def sum_of(u, h):
        part, _, side, _ = bufs(u)
        a, b = pl.ds(*ra), pl.ds(*rb)
        got(u, side.at[h, 0, b], 6 * h + 2)
        got(u, side.at[h, 1, a], 6 * h + 3)
        got(u, side.at[h, 0, a], 6 * h + 4)
        got(u, side.at[h, 1, b], 6 * h + 5)
        own = me.in_narrow(0, h)
        return part[own].astype(F32) + side[h, 0].astype(F32) + side[h, 1].astype(F32)

    def scatter_across(u):
        zbuf = bufs(u)[3]
        zbuf[0] = sum_of(u, 1).astype(BF16)
        put(u, zbuf.at[0], zbuf.at[1], 12, across)

    def finish(u):
        kind, t = u
        zbuf = bufs(u)[3]
        summed = sum_of(u, 0)
        got(u, zbuf.at[1], 12)
        summed = summed + zbuf[1].astype(F32)
        mine = result(u, me.narrow, whole)
        if kind == "q":
            v = summed + qkv_bias
            turned = v[:, :ROT_COLS]
            turned = (
                turned * tables[t, 0]
                + pltpu.roll(turned, ROT_COLS - ROTARY // 2, 1) * tables[t, 1]
                + pltpu.roll(turned, ROTARY // 2, 1) * tables[t, 2]
            )
            qkv[me.narrow * 2 + side_of(t)] = jnp.concatenate([turned, v[:, ROT_COLS:]], axis=1).astype(BF16)
        else:
            v = summed + up_bias
            units[me.narrow * 2 + side_of(t)] = (0.5 * v * (1.0 + lax.erf(v * (0.5**0.5)))).astype(BF16)
        put(u, mine, mine, 13, across)
        put(u, mine, mine, 14, up)
        put(u, mine, mine, 15, down)

    def relay_half(u, h):
        below, above = me.in_narrow(3, h), me.in_narrow(1, h)
        got(u, result(u, below, whole), 14 + 4 * h)
        put(u, result(u, below, ra), result(u, below, ra), 16 + 4 * h, up)
        got(u, result(u, above, whole), 15 + 4 * h)
        put(u, result(u, above, rb), result(u, above, rb), 17 + 4 * h, down)

    def relay_across(u):
        block = result(u, me.in_narrow(0, 1), whole)
        got(u, block, 13)
        put(u, block, block, 18, up)
        put(u, block, block, 19, down)

    def gather_last(u):
        for h in range(2):
            far = me.in_narrow(2, h)
            got(u, result(u, far, ra), 16 + 4 * h)
            got(u, result(u, far, rb), 17 + 4 * h)

    q0, q1, u0, u1 = ("q", 0), ("q", 1), ("u", 0), ("u", 1)
    gather_first()
    multiply(*q0)
    scatter_first(q0)
    multiply(*u0)
    scatter_second(q0)
    scatter_first(u0)
    gather_second()
    rotation_factors()
    multiply(*q1)
    scatter_second(u0)
    scatter_first(q1)
    multiply(*u1)
    scatter_across(q0)
    scatter_second(q1)
    scatter_first(u1)
    finish(q0)
    scatter_across(u0)
    scatter_second(u1)
    scatter_across(q1)
    finish(u0)
    relay_half(q0, 0)
    relay_across(q0)
    finish(q1)
    scatter_across(u1)
    relay_half(u0, 0)
    relay_across(u0)
    relay_half(q0, 1)
    relay_half(q1, 0)
    finish(u1)
    relay_across(q1)
    relay_half(u0, 1)
    relay_half(q1, 1)
    relay_half(u1, 0)
    relay_across(u1)
    relay_half(u1, 1)
    for u in (q0, q1, u0, u1):
        gather_last(u)
    for copy in open_copies:
        copy.wait_send()


def attend_kernel(lens, sinks, pages, qkv_ref, out_ref, cache_ref):
    block = pl.program_id(0)
    queries, span, tail = 256, 384, 128
    total = qkv_ref.shape[0]
    first = block * queries
    width = out_ref.shape[1]

    def of_sequence(token):
        end = 0
        start = jnp.zeros_like(token)
        sink = jnp.zeros_like(token) + sinks[0]
        for s in range(8):
            end = end + lens[s]
            after = token >= end
            start = jnp.where(after, end, start)
            if s < 7:
                sink = jnp.where(after, sinks[s + 1], sink)
        return start, start + sink

    query = first + lax.broadcasted_iota(jnp.int32, (queries, 1), 0)
    start, sink_end = of_sequence(query)
    near = pl.multiple_of(jnp.maximum(first - WINDOW, 0), WINDOW)
    head_start, _ = of_sequence(first)
    far = pl.multiple_of(jnp.minimum(head_start // 16 * 16, total - tail), 16)
    near_key = near + lax.broadcasted_iota(jnp.int32, (1, span), 1)
    far_key = far + lax.broadcasted_iota(jnp.int32, (1, tail), 1)

    def allowed(key):
        return (key >= start) & (key <= query) & ((query - key < WINDOW) | (key < sink_end))

    near_ok = allowed(near_key)
    far_ok = allowed(far_key) & (far_key < near)
    mask = jnp.concatenate([near_ok, far_ok], axis=1)
    q = qkv_ref[pl.ds(first, queries), :][:, :width]
    near_rows = qkv_ref[pl.ds(near, span), :]
    far_rows = qkv_ref[pl.ds(far, tail), :]
    keys = jnp.concatenate([near_rows[:, width : 2 * width], far_rows[:, width : 2 * width]], axis=0)
    values = jnp.concatenate(
        [near_rows[:, 2 * width : 3 * width], far_rows[:, 2 * width : 3 * width]], axis=0
    )
    lane = lax.broadcasted_iota(jnp.int32, (queries, width), 1)
    result = None
    for head in range(width // HEAD_DIM):
        in_head = (lane >= head * HEAD_DIM) & (lane < (head + 1) * HEAD_DIM)
        masked_q = jnp.where(in_head, q, jnp.zeros_like(q))
        scores = lax.dot_general(
            masked_q, keys, (((1,), (1,)), ((), ())), preferred_element_type=F32
        ) * (1.0 / HEAD_DIM**0.5)
        scores = jnp.where(mask, scores, F32(-1e30))
        weights = jnp.exp(scores - jnp.max(scores, axis=1, keepdims=True))
        probs = (weights * (1.0 / jnp.sum(weights, axis=1, keepdims=True))).astype(BF16)
        got = jnp.dot(probs, values, preferred_element_type=F32)
        result = got if result is None else jnp.where(in_head, got, result)
    out_ref[...] = result.astype(BF16)
    for j in range(2):
        row = pl.multiple_of(pages[block * 2 + j] * PAGE, PAGE)
        page = qkv_ref[pl.ds(row, PAGE), :]
        cache_ref[0, j] = page[:, width : 2 * width]
        cache_ref[1, j] = page[:, 2 * width : 3 * width]


def attend(lens, sinks, pages, qkv, width):
    return pl.pallas_call(
        attend_kernel,
        out_shape=[
            jax.ShapeDtypeStruct((qkv.shape[0], width), BF16),
            jax.ShapeDtypeStruct((2, 16, PAGE, width), BF16),
        ],
        grid_spec=pltpu.PrefetchScalarGridSpec(
            num_scalar_prefetch=3,
            grid=(8,),
            in_specs=[pl.BlockSpec(qkv.shape, lambda b, *_: (0, 0))],
            out_specs=[
                pl.BlockSpec((256, width), lambda b, *_: (b, 0)),
                pl.BlockSpec((2, 2, PAGE, width), lambda b, *_: (0, b, 0, 0)),
            ],
        ),
        name="attend",
    )(lens, sinks, pages, qkv)


def output_kernel(
    att_ref,
    units_ref,
    w_out_ref,
    w_down_ref,
    hidden_ref,
    bias_ref,
    out_ref,
    products,
    core_in,
    halves,
    x_in,
    z_out,
    z_in,
    core_send,
    core_recv,
    x_send,
    x_recv,
    z_send,
    z_recv,
):
    me = Place()
    greet([me.wide_peer(*hop) for hop in WIDE_HOPS])
    open_copies = []
    sibling = me.wide_peer(0, 0, 1)
    width = out_ref.shape[1]
    order = (2, 1, 3, 0)
    for half in range(2):
        for dx in order:
            n = lax.rem(me.x + dx, 4) * 2 + half
            o = jnp.dot(units_ref[n], w_down_ref[...], preferred_element_type=F32)
            o = o + jnp.dot(att_ref[n], w_out_ref[...], preferred_element_type=F32)
            products[n] = o.astype(BF16).reshape(2, 2, 64, width)
            for j in range(2):
                i = half * 8 + dx * 2 + j
                open_copies.append(
                    send(
                        products.at[n, j, 1 - me.c], core_in.at[n, j], core_send.at[i], core_recv.at[i], sibling
                    )
                )
    for half in range(2):
        for dx in order:
            n = lax.rem(me.x + dx, 4) * 2 + half
            for j in range(2):
                arrived(core_in.at[n, j], core_recv.at[half * 8 + dx * 2 + j], sibling)
            halves[half, dx] = (products[n, :, me.c].astype(F32) + core_in[n].astype(F32)).astype(BF16)
            if dx:
                i = half * 3 + dx - 1
                there = half * 3 + (4 - dx) - 1
                open_copies.append(
                    send(
                        halves.at[half, dx], x_in.at[half, 3 - dx],
                        x_send.at[i], x_recv.at[there], me.wide_peer(dx, 0, 0),
                    )
                )
    for half in range(2):
        total = halves[half, 0].astype(F32)
        for dx in (1, 3, 2):
            arrived(x_in.at[half, dx - 1], x_recv.at[half * 3 + dx - 1], sibling)
            total = total + x_in[half, dx - 1].astype(F32)
        z_out[half] = total.astype(BF16)
        for j in range(2):
            to = half * 2 + j
            peer = {"wide": me.x * 8 + to * 2 + me.c, "narrow": me.narrow}

            @pl.when(me.zl != to)
            def _():
                send(z_out.at[half, j], z_in.at[me.zl], z_send.at[to], z_recv.at[me.zl], peer)

    total = z_out[me.zl // 2, me.zl % 2].astype(F32) + hidden_ref[...].astype(F32) + bias_ref[...].reshape(1, FEAT)
    for k in range(1, 4):
        source = lax.rem(me.zl + k, 4)
        arrived(z_in.at[source], z_recv.at[source], sibling)
        total = total + z_in[source].astype(F32)
    out_ref[...] = total.astype(BF16)
    for copy in open_copies:
        copy.wait_send()
    for k in range(1, 4):
        to = lax.rem(me.zl + k, 4)
        pltpu.make_async_remote_copy(
            src_ref=z_out.at[to // 2, to % 2], dst_ref=z_in.at[me.zl], send_sem=z_send.at[to],
            recv_sem=z_recv.at[me.zl], device_id=me.wide_peer(0, k, 0), device_id_type=MESH,
        ).wait_send()


def output(att, units, w_out, w_down, hidden, bias):
    width = hidden.shape[1]
    return pl.pallas_call(
        output_kernel,
        out_shape=jax.ShapeDtypeStruct(hidden.shape, BF16),
        in_specs=[pl.BlockSpec(memory_space=VM)] * 6,
        out_specs=pl.BlockSpec(memory_space=VM),
        scratch_shapes=[
            VM((8, 2, 2, 64, width), BF16),
            VM((8, 2, 64, width), BF16),
            VM((2, 4, 2, 64, width), BF16),
            VM((2, 3, 2, 64, width), BF16),
            VM((2, 2, 64, width), BF16),
            VM((4, 64, width), BF16),
            DMA((16,)),
            DMA((16,)),
            DMA((6,)),
            DMA((6,)),
            DMA((4,)),
            DMA((4,)),
        ],
        compiler_params=pltpu.CompilerParams(
            collective_id=1, has_side_effects=True, vmem_limit_bytes=56 << 20
        ),
        name="output",
    )(att, units, w_out, w_down, hidden, bias)


def local(
    hidden_in,
    w_query,
    w_key,
    w_value,
    qkv_bias,
    w_up,
    up_bias,
    w_attn_out,
    w_down,
    out_bias,
    norm_gain,
    norm_bias,
    seq_lens,
    sink_count,
    page_table,
):
    vmem = pl.BlockSpec(memory_space=VM)
    smem = pl.BlockSpec(memory_space=pltpu.SMEM)
    both = (QKV_PAD, QKV_PAD, UNITS, UNITS)
    qkv, units = pl.pallas_call(
        project_kernel,
        out_shape=[jax.ShapeDtypeStruct((TOKENS // OWN, OWN, c), BF16) for c in (QKV_PAD, UNITS)],
        in_specs=[smem] + [vmem] * 9,
        out_specs=[vmem] * 2,
        scratch_shapes=[
            VM((FEAT, QKV_PAD), BF16),
            VM((32, BLOCK, FEAT), BF16),
            VM((32, 8, 128), F32),
            VM((8, 8, 128), F32),
            VM((2, 3, OWN, ROT_COLS), F32),
            VM((2, 2, 8, 2, BLOCK, FEAT), BF16),
        ]
        + [VM((8, OWN, c), BF16) for c in both]
        + [VM((2, 2, OWN // 2, c), BF16) for c in both]
        + [VM((2, 2, OWN, c), BF16) for c in both]
        + [VM((2, OWN, c), BF16) for c in both]
        + [
            DMA((31,)),
            DMA((32,)),
            DMA((31,)),
            DMA((32,)),
            DMA((7,)),
            DMA((8,)),
            DMA((4, 22)),
            DMA((4, 22)),
        ],
        compiler_params=pltpu.CompilerParams(
            collective_id=0, has_side_effects=True, vmem_limit_bytes=56 << 20
        ),
        name="project",
    )(
        seq_lens,
        hidden_in,
        norm_gain,
        norm_bias,
        w_query.T,
        w_key.T,
        w_value.T,
        w_up,
        qkv_bias,
        up_bias,
    )
    slot_ids = lax.axis_index("narrow") * 16 + jnp.arange(16, dtype=jnp.int32)
    matches = (page_table[None, :] == slot_ids[:, None]).astype(jnp.int32)
    source_page = jnp.sum(matches * jnp.arange(NPAGES, dtype=jnp.int32)[None, :], axis=1)
    attended, cache = attend(seq_lens, sink_count, source_page, qkv.reshape(TOKENS, QKV_PAD), HEADS2)
    hidden_out = output(
        attended.reshape(8, 2 * OWN, HEADS2), units.reshape(8, 2 * OWN, UNITS), w_attn_out, w_down, hidden_in, out_bias
    )
    return (hidden_out, cache)


def solution(mesh):
    in_specs = (
        P("wide", "narrow"),
        P("narrow", "wide"),
        P("narrow", "wide"),
        P("narrow", "wide"),
        P(None, "wide"),
        P("narrow", "wide"),
        P("wide"),
        P("wide", "narrow"),
        P("wide", "narrow"),
        P("narrow"),
        P(None, "narrow"),
        P(None, "narrow"),
        P(),
        P(),
        P(),
    )
    out_specs = (P("wide", "narrow"), P(None, "narrow", None, "wide"))
    return jax.shard_map(local, mesh=mesh, in_specs=in_specs, out_specs=out_specs, check_vma=False)
```

```python
import jax
import jax.numpy as jnp
import numpy as np
from jax import lax
from jax.experimental import pallas as pl
from jax.experimental.pallas import tpu as pltpu
from jax.sharding import PartitionSpec as P

D = 6144
HEAD_DIM = 96
ROTARY = 24
PAGE = 16
WINDOW = 128
SEQS = 8
NPAGES = 128
TOKENS = 2048
MESH = pl.DeviceIdType.MESH
F32 = jnp.float32
BF16 = jnp.bfloat16
VM = pltpu.VMEM
DMA = pltpu.SemaphoreType.DMA
FEAT = 768
HEADS2 = 192
ROT_COLS = 2 * HEADS2
QKV_PAD = 640
UNITS = 768
BLOCK = 64
OWN = 128
COLS = {"q": QKV_PAD, "u": UNITS}


class Place:
    def __init__(self):
        wide = lax.axis_index("wide")
        narrow = lax.axis_index("narrow")
        self.x, self.zl, self.c = wide // 8, (wide // 2) % 4, wide % 2
        self.y, self.zh = narrow // 2, narrow % 2
        self.wide, self.narrow = wide, narrow

    def in_wide(self, dx, dz, dc):
        return lax.rem(self.x + dx, 4) * 8 + lax.rem(self.zl + dz, 4) * 2 + lax.rem(self.c + dc, 2)

    def in_narrow(self, dy, dh):
        return lax.rem(self.y + dy, 4) * 2 + lax.rem(self.zh + dh, 2)

    def wide_peer(self, dx, dz, dc):
        return {"wide": self.in_wide(dx, dz, dc), "narrow": self.narrow}

    def narrow_peer(self, dy, dh):
        return {"wide": self.wide, "narrow": self.in_narrow(dy, dh)}


def greet(peers):
    barrier = pltpu.get_barrier_semaphore()
    for peer in peers:
        pl.semaphore_signal(barrier, inc=1, device_id=peer, device_id_type=MESH)
    pl.semaphore_wait(barrier, len(peers))


def send(src, dst, send_sem, recv_sem, peer):
    copy = pltpu.make_async_remote_copy(
        src_ref=src,
        dst_ref=dst,
        send_sem=send_sem,
        recv_sem=recv_sem,
        device_id=peer,
        device_id_type=MESH,
    )
    copy.start()
    return copy


def arrived(dst, sem, peer):
    pltpu.make_async_remote_copy(
        src_ref=dst, dst_ref=dst, send_sem=sem, recv_sem=sem, device_id=peer, device_id_type=MESH
    ).wait_recv()


WIDE_HOPS = [(0, 2, 0), (1, 0, 0), (3, 0, 0), (2, 0, 0), (0, 1, 0), (0, 3, 0), (0, 0, 1)]
NARROW_HOPS = [(dy, dh) for dy in range(4) for dh in range(2) if dy or dh]
KINDS = ("q", "u")


def slot(a, k, c):
    return (a % 4) * 8 + (k % 4) * 2 + c % 2


def project_kernel(
    lens,
    hidden_ref,
    gain_ref,
    shift_ref,
    w_query,
    w_key,
    w_value,
    w_up,
    qkv_bias_ref,
    up_bias_ref,
    qkv,
    units,
    w_qkv,
    gathered,
    stats,
    stats_part,
    tables,
    normed,
    part_q0,
    part_q1,
    part_u0,
    part_u1,
    first_q0,
    first_q1,
    first_u0,
    first_u1,
    side_q0,
    side_q1,
    side_u0,
    side_u1,
    across_q0,
    across_q1,
    across_u0,
    across_u1,
    wide_send,
    wide_recv,
    stat_send,
    stat_recv,
    sn_send,
    sn_recv,
    unit_send,
    unit_recv,
):
    parts = {"q": (part_q0, part_q1), "u": (part_u0, part_u1)}
    firsts = {"q": (first_q0, first_q1), "u": (first_u0, first_u1)}
    sides = {"q": (side_q0, side_q1), "u": (side_u0, side_u1)}
    acrosses = {"q": (across_q0, across_q1), "u": (across_u0, across_u1)}
    me = Place()
    parity = me.zl % 2
    sibling = me.wide_peer(0, 0, 1)
    greet([me.wide_peer(*hop) for hop in WIDE_HOPS] + [me.narrow_peer(*hop) for hop in NARROW_HOPS])
    open_copies = []

    counts = {"wide": 0, "stat": 0}

    def push(kind, rel, hop, own=False):
        buf, ss, rs = (
            (gathered, wide_send, wide_recv) if kind == "wide" else (stats, stat_send, stat_recv)
        )
        i = counts[kind]
        counts[kind] = i + 1
        index = me.in_wide(*rel)
        src = hidden_ref if own and kind == "wide" else buf.at[index]
        there = slot(rel[0] - hop[0], rel[1] - hop[1], rel[2] - hop[2])
        open_copies.append(send(src, buf.at[index], ss.at[i], rs.at[there], me.wide_peer(*hop)))

    def wait_block(kind, rel):
        buf, rs = (gathered, wide_recv) if kind == "wide" else (stats, stat_recv)
        arrived(buf.at[me.in_wide(*rel)], rs.at[slot(*rel)], sibling)

    def normalise(block, rel):
        index = me.in_wide(*rel)
        as_float = block.astype(F32)
        line = stats[index][0:1, :]
        lane = lax.broadcasted_iota(jnp.int32, (BLOCK, 128), 1)
        row = lax.broadcasted_iota(jnp.int32, (BLOCK, 128), 0)
        average = jnp.sum(jnp.where(lane == row, line, 0.0), axis=1, keepdims=True)
        inverse = jnp.sum(jnp.where(lane == row + BLOCK, line, 0.0), axis=1, keepdims=True)
        scaled = (as_float - average) * inverse
        owner = lax.rem(me.x + rel[0], 4) * 2 + lax.rem(me.zl + rel[1], 4) // 2
        core = lax.rem(me.c + rel[2], 2)
        for i in range(2):
            normed[i, rel[1] % 2, owner, core] = (
                scaled * gain_ref[i : i + 1, :] + shift_ref[i : i + 1, :]
            ).astype(BF16)

    own, core_hop = (0, 0, 0), (0, 0, 1)
    x_hops = [(1, 0, 0), (3, 0, 0), (2, 0, 0)]
    for hop in [(0, 2, 0)] + x_hops + [core_hop]:
        push("wide", own, hop, True)
    lanes = lax.broadcasted_iota(jnp.int32, (BLOCK, 128), 1)
    rows = lax.broadcasted_iota(jnp.int32, (BLOCK, 128), 0)
    as_float = hidden_ref[...].astype(F32)
    sums = jnp.sum(as_float, axis=1, keepdims=True)
    squares = jnp.sum(as_float * as_float, axis=1, keepdims=True)
    line = jnp.where(lanes == rows, sums, 0.0) + jnp.where(lanes == rows + BLOCK, squares, 0.0)
    stats_part[me.narrow] = jnp.broadcast_to(jnp.sum(line, axis=0, keepdims=True), (8, 128))
    for i, (dy, dh) in enumerate(NARROW_HOPS):
        mine = stats_part.at[me.narrow]
        there = ((-dy) % 4) * 2 + (-dh) % 2
        open_copies.append(send(mine, mine, sn_send.at[i], sn_recv.at[there], me.narrow_peer(dy, dh)))
    for hop in [(0, 1, 0), (0, 3, 0)]:
        push("wide", own, hop, True)
    rel = (0, 2, 0)
    wait_block("wide", rel)
    for hop in x_hops + [core_hop]:
        push("wide", rel, hop)
    for dy, dh in NARROW_HOPS:
        arrived(stats_part.at[me.in_narrow(dy, dh)], sn_recv.at[dy * 2 + dh], sibling)
    total = stats_part[0]
    for i in range(1, 8):
        total = total + stats_part[i]
    average = total[:, :BLOCK] / D
    variance = total[:, BLOCK:] / D - average * average
    stats[me.wide] = jnp.concatenate([average, lax.rsqrt(variance + 1e-05)], axis=1)
    for hop in WIDE_HOPS:
        push("stat", own, hop, True)
    normalise(hidden_ref[...], own)
    wait_block("stat", rel)
    for hop in x_hops + [core_hop]:
        push("stat", rel, hop)
    normalise(gathered[me.in_wide(*rel)], rel)

    pad = QKV_PAD - 3 * HEADS2
    qkv_bias = jnp.concatenate(
        [qkv_bias_ref[i : i + 1, :] for i in range(3)] + [jnp.zeros((1, pad), F32)], axis=1
    )
    up_bias = up_bias_ref[...].reshape(1, UNITS)
    w_qkv[...] = jnp.concatenate(
        [w_query[...], w_key[...], w_value[...], jnp.zeros((pad, FEAT), BF16)], axis=0
    ).T

    def sequence_start(token):
        end = 0
        start = token * 0
        for s in range(SEQS):
            end = end + lens[s]
            start = jnp.where(token >= end, end, start)
        return start

    def side_of(t):
        return parity if t == 0 else 1 - parity

    def first_token(t, owner):
        return owner * (2 * OWN) + side_of(t) * OWN

    def rotation_factors():
        lane = lax.broadcasted_iota(jnp.int32, (1, ROT_COLS), 1) % HEAD_DIM
        step = lane % (ROTARY // 2)
        inverses = np.power(np.float32(10000.0), (-2.0 * np.arange(12) / ROTARY).astype(np.float32))
        frequency = jnp.zeros((1, ROT_COLS), F32)
        for i in range(ROTARY // 2):
            frequency = jnp.where(step == i, F32(inverses[i]), frequency)
        for t in range(2):
            token = first_token(t, me.narrow) + lax.broadcasted_iota(jnp.int32, (OWN, 1), 0)
            position = (token - sequence_start(token)).astype(F32)
            angle = jnp.where(lane < ROTARY, position * frequency, 0.0)
            sine = jnp.sin(angle)
            tables[t, 0] = jnp.cos(angle)
            tables[t, 1] = jnp.where(lane < ROTARY // 2, -sine, 0.0)
            tables[t, 2] = jnp.where(lane < ROTARY // 2, 0.0, sine)

    def from_x(k, a):
        rel = (a, k, 0)
        for kind in ("wide", "stat"):
            wait_block(kind, rel)
            push(kind, rel, core_hop)
        normalise(gathered[me.in_wide(*rel)], rel)

    def from_sibling(ks):
        for k in ks:
            for a in (0, 1, 3, 2):
                rel = (a, k, 1)
                for kind in ("wide", "stat"):
                    wait_block(kind, rel)
                normalise(gathered[me.in_wide(*rel)], rel)

    def gather_first():
        for a in (1, 3, 2):
            from_x(0, a)
        for k in (1, 3):
            rel = (0, k, 0)
            wait_block("stat", rel)
            for hop in x_hops + [core_hop]:
                push("stat", rel, hop)
            wait_block("wide", rel)
            push("wide", rel, core_hop)
        for a in (1, 3):
            from_x(2, a)
        for k in (1, 3):
            for hop in x_hops:
                push("wide", (0, k, 0), hop)
        from_x(2, 2)
        from_sibling((0, 2))

    def gather_second():
        for k in (1, 3):
            normalise(gathered[me.in_wide(0, k, 0)], (0, k, 0))
        for k in (1, 3):
            for a in (1, 3, 2):
                from_x(k, a)
        from_sibling((1, 3))

    def multiply(kind, t):
        which, weight = (0, w_qkv) if kind == "q" else (1, w_up)
        part = parts[kind][t]

        @pl.loop(0, 4)
        def _(pair):
            rows = normed[which, t, pl.ds(pair * 2, 2)].reshape(2 * OWN, FEAT)
            product = jnp.dot(rows, weight[...], preferred_element_type=F32).astype(BF16)
            part[pl.ds(pair * 2, 2)] = product.reshape(2, OWN, COLS[kind])

    sent = {}
    up, down, across = me.narrow_peer(1, 0), me.narrow_peer(3, 0), me.narrow_peer(0, 1)
    whole, ra, rb = (0, OWN), (0, OWN // 2), (OWN // 2, OWN // 2)

    def number(u):
        return KINDS.index(u[0]) * 2 + u[1]

    def put(u, src, dst, sem, peer):
        i = sent.get(u, 0)
        sent[u] = i + 1
        n = number(u)
        open_copies.append(send(src, dst, unit_send.at[n, i], unit_recv.at[n, sem], peer))

    def got(u, dst, sem):
        arrived(dst, unit_recv.at[number(u), sem], up)

    def bufs(u):
        kind, t = u
        return parts[kind][t], firsts[kind][t], sides[kind][t], acrosses[kind][t]

    def result(u, owner, rows):
        kind, t = u
        if kind == "q":
            return qkv.at[owner * 2 + side_of(t), pl.ds(*rows)]
        return units.at[owner * 2 + side_of(t), pl.ds(*rows)]

    def scatter_first(u):
        part, first, side, _ = bufs(u)
        for h in (1, 0):
            far, nxt, prv = me.in_narrow(2, h), me.in_narrow(1, h), me.in_narrow(3, h)
            a, b = pl.ds(*ra), pl.ds(*rb)
            put(u, part.at[far, a], first.at[h, 0], 6 * h + 0, up)
            put(u, part.at[far, b], first.at[h, 1], 6 * h + 1, down)
            put(u, part.at[nxt, b], side.at[h, 0, b], 6 * h + 2, up)
            put(u, part.at[prv, a], side.at[h, 1, a], 6 * h + 3, down)

    def scatter_second(u):
        part, first, side, _ = bufs(u)
        a, b = pl.ds(*ra), pl.ds(*rb)
        for h in (1, 0):
            nxt, prv = me.in_narrow(1, h), me.in_narrow(3, h)
            got(u, first.at[h, 0], 6 * h + 0)
            part[nxt, a] = (part[nxt, a].astype(F32) + first[h, 0].astype(F32)).astype(BF16)
            put(u, part.at[nxt, a], side.at[h, 0, a], 6 * h + 4, up)
            got(u, first.at[h, 1], 6 * h + 1)
            part[prv, b] = (part[prv, b].astype(F32) + first[h, 1].astype(F32)).astype(BF16)
            put(u, part.at[prv, b], side.at[h, 1, b], 6 * h + 5, down)

    def sum_of(u, h):
        part, _, side, _ = bufs(u)
        a, b = pl.ds(*ra), pl.ds(*rb)
        got(u, side.at[h, 0, b], 6 * h + 2)
        got(u, side.at[h, 1, a], 6 * h + 3)
        got(u, side.at[h, 0, a], 6 * h + 4)
        got(u, side.at[h, 1, b], 6 * h + 5)
        own = me.in_narrow(0, h)
        return part[own].astype(F32) + side[h, 0].astype(F32) + side[h, 1].astype(F32)

    def scatter_across(u):
        zbuf = bufs(u)[3]
        zbuf[0] = sum_of(u, 1).astype(BF16)
        put(u, zbuf.at[0], zbuf.at[1], 12, across)

    def finish(u):
        kind, t = u
        zbuf = bufs(u)[3]
        summed = sum_of(u, 0)
        got(u, zbuf.at[1], 12)
        summed = summed + zbuf[1].astype(F32)
        mine = result(u, me.narrow, whole)
        if kind == "q":
            v = summed + qkv_bias
            turned = v[:, :ROT_COLS]
            turned = (
                turned * tables[t, 0]
                + pltpu.roll(turned, ROT_COLS - ROTARY // 2, 1) * tables[t, 1]
                + pltpu.roll(turned, ROTARY // 2, 1) * tables[t, 2]
            )
            qkv[me.narrow * 2 + side_of(t)] = jnp.concatenate([turned, v[:, ROT_COLS:]], axis=1).astype(BF16)
        else:
            v = summed + up_bias
            units[me.narrow * 2 + side_of(t)] = (0.5 * v * (1.0 + lax.erf(v * (0.5**0.5)))).astype(BF16)
        put(u, mine, mine, 13, across)
        put(u, mine, mine, 14, up)
        put(u, mine, mine, 15, down)

    def relay_half(u, h):
        below, above = me.in_narrow(3, h), me.in_narrow(1, h)
        got(u, result(u, below, whole), 14 + 4 * h)
        put(u, result(u, below, ra), result(u, below, ra), 16 + 4 * h, up)
        got(u, result(u, above, whole), 15 + 4 * h)
        put(u, result(u, above, rb), result(u, above, rb), 17 + 4 * h, down)

    def relay_across(u):
        block = result(u, me.in_narrow(0, 1), whole)
        got(u, block, 13)
        put(u, block, block, 18, up)
        put(u, block, block, 19, down)

    def gather_last(u):
        for h in range(2):
            far = me.in_narrow(2, h)
            got(u, result(u, far, ra), 16 + 4 * h)
            got(u, result(u, far, rb), 17 + 4 * h)

    q0, q1, u0, u1 = ("q", 0), ("q", 1), ("u", 0), ("u", 1)
    gather_first()
    multiply(*q0)
    scatter_first(q0)
    multiply(*u0)
    scatter_second(q0)
    scatter_first(u0)
    gather_second()
    rotation_factors()
    multiply(*q1)
    scatter_second(u0)
    scatter_first(q1)
    multiply(*u1)
    scatter_across(q0)
    scatter_second(q1)
    scatter_first(u1)
    finish(q0)
    scatter_across(u0)
    scatter_second(u1)
    scatter_across(q1)
    finish(u0)
    relay_half(q0, 0)
    relay_across(q0)
    finish(q1)
    scatter_across(u1)
    relay_half(u0, 0)
    relay_across(u0)
    relay_half(q0, 1)
    relay_half(q1, 0)
    finish(u1)
    relay_across(q1)
    relay_half(u0, 1)
    relay_half(q1, 1)
    relay_half(u1, 0)
    relay_across(u1)
    relay_half(u1, 1)
    for u in (q0, q1, u0, u1):
        gather_last(u)
    for copy in open_copies:
        copy.wait_send()


def attend_kernel(lens, sinks, pages, qkv_ref, out_ref, cache_ref):
    block = pl.program_id(0)
    queries, span, tail = 256, 384, 128
    total = qkv_ref.shape[0]
    first = block * queries
    width = out_ref.shape[1]

    def of_sequence(token):
        end = 0
        start = jnp.zeros_like(token)
        sink = jnp.zeros_like(token) + sinks[0]
        for s in range(8):
            end = end + lens[s]
            after = token >= end
            start = jnp.where(after, end, start)
            if s < 7:
                sink = jnp.where(after, sinks[s + 1], sink)
        return start, start + sink

    query = first + lax.broadcasted_iota(jnp.int32, (queries, 1), 0)
    start, sink_end = of_sequence(query)
    near = pl.multiple_of(jnp.maximum(first - WINDOW, 0), WINDOW)
    head_start, _ = of_sequence(first)
    far = pl.multiple_of(jnp.minimum(head_start // 16 * 16, total - tail), 16)
    near_key = near + lax.broadcasted_iota(jnp.int32, (1, span), 1)
    far_key = far + lax.broadcasted_iota(jnp.int32, (1, tail), 1)

    far_key = jnp.where(far_key < near, far_key, 2 * total)
    key = jnp.concatenate([near_key, far_key], axis=1)
    mask = (key <= query) & (key >= start) & ((key > query - WINDOW) | (key < sink_end))
    q = qkv_ref[pl.ds(first, queries), :][:, :width]
    near_rows = qkv_ref[pl.ds(near, span), :]
    far_rows = qkv_ref[pl.ds(far, tail), :]
    keys = jnp.concatenate([near_rows[:, width : 2 * width], far_rows[:, width : 2 * width]], axis=0)
    values = jnp.concatenate(
        [near_rows[:, 2 * width : 3 * width], far_rows[:, 2 * width : 3 * width]], axis=0
    )
    lane = lax.broadcasted_iota(jnp.int32, (queries, width), 1)
    result = None
    for head in range(width // HEAD_DIM):
        in_head = (lane >= head * HEAD_DIM) & (lane < (head + 1) * HEAD_DIM)
        masked_q = jnp.where(in_head, q, jnp.zeros_like(q))
        scores = lax.dot_general(
            masked_q, keys, (((1,), (1,)), ((), ())), preferred_element_type=F32
        ) * (1.0 / HEAD_DIM**0.5)
        scores = jnp.where(mask, scores, F32(-1e30))
        weights = jnp.exp(scores - jnp.max(scores, axis=1, keepdims=True))
        probs = (weights * (1.0 / jnp.sum(weights, axis=1, keepdims=True))).astype(BF16)
        got = jnp.dot(probs, values, preferred_element_type=F32)
        result = got if result is None else jnp.where(in_head, got, result)
    out_ref[...] = result.astype(BF16)
    for j in range(2):
        row = pl.multiple_of(pages[block * 2 + j] * PAGE, PAGE)
        page = qkv_ref[pl.ds(row, PAGE), :]
        cache_ref[0, j] = page[:, width : 2 * width]
        cache_ref[1, j] = page[:, 2 * width : 3 * width]


def attend(lens, sinks, pages, qkv, width):
    return pl.pallas_call(
        attend_kernel,
        out_shape=[
            jax.ShapeDtypeStruct((qkv.shape[0], width), BF16),
            jax.ShapeDtypeStruct((2, 16, PAGE, width), BF16),
        ],
        grid_spec=pltpu.PrefetchScalarGridSpec(
            num_scalar_prefetch=3,
            grid=(8,),
            in_specs=[pl.BlockSpec(qkv.shape, lambda b, *_: (0, 0))],
            out_specs=[
                pl.BlockSpec((256, width), lambda b, *_: (b, 0)),
                pl.BlockSpec((2, 2, PAGE, width), lambda b, *_: (0, b, 0, 0)),
            ],
        ),
        name="attend",
    )(lens, sinks, pages, qkv)


def output_kernel(
    att_ref,
    units_ref,
    w_out_ref,
    w_down_ref,
    hidden_ref,
    bias_ref,
    out_ref,
    products,
    core_in,
    halves,
    x_in,
    z_out,
    z_in,
    core_send,
    core_recv,
    x_send,
    x_recv,
    z_send,
    z_recv,
):
    me = Place()
    greet([me.wide_peer(*hop) for hop in WIDE_HOPS])
    open_copies = []
    sibling = me.wide_peer(0, 0, 1)
    width = out_ref.shape[1]
    order = (2, 1, 3, 0)

    def multiply(half, dx):
        n = lax.rem(me.x + dx, 4) * 2 + half
        o = jnp.dot(units_ref[n], w_down_ref[...], preferred_element_type=F32)
        o = o + jnp.dot(att_ref[n], w_out_ref[...], preferred_element_type=F32)
        products[n] = o.astype(BF16).reshape(2, 2, 64, width)
        for j in range(2):
            i = half * 8 + dx * 2 + j
            open_copies.append(
                send(
                    products.at[n, j, 1 - me.c], core_in.at[n, j], core_send.at[i], core_recv.at[i], sibling
                )
            )

    def pass_on(half, dx):
        n = lax.rem(me.x + dx, 4) * 2 + half
        for j in range(2):
            arrived(core_in.at[n, j], core_recv.at[half * 8 + dx * 2 + j], sibling)
        halves[half, dx] = (products[n, :, me.c].astype(F32) + core_in[n].astype(F32)).astype(BF16)
        if dx:
            i = half * 3 + dx - 1
            there = half * 3 + (4 - dx) - 1
            open_copies.append(
                send(
                    halves.at[half, dx],
                    x_in.at[half, 3 - dx],
                    x_send.at[i],
                    x_recv.at[there],
                    me.wide_peer(dx, 0, 0),
                )
            )

    steps = [(half, dx) for half in range(2) for dx in order]
    for i, step in enumerate(steps):
        multiply(*step)
        if i:
            pass_on(*steps[i - 1])
    pass_on(*steps[-1])
    for half in range(2):
        total = halves[half, 0].astype(F32)
        for dx in (1, 3, 2):
            arrived(x_in.at[half, dx - 1], x_recv.at[half * 3 + dx - 1], sibling)
            total = total + x_in[half, dx - 1].astype(F32)
        z_out[half] = total.astype(BF16)
        for j in range(2):
            to = half * 2 + j
            peer = {"wide": me.x * 8 + to * 2 + me.c, "narrow": me.narrow}

            @pl.when(me.zl != to)
            def _():
                send(z_out.at[half, j], z_in.at[me.zl], z_send.at[to], z_recv.at[me.zl], peer)

    total = z_out[me.zl // 2, me.zl % 2].astype(F32) + hidden_ref[...].astype(F32) + bias_ref[...].reshape(1, FEAT)
    for k in range(1, 4):
        source = lax.rem(me.zl + k, 4)
        arrived(z_in.at[source], z_recv.at[source], sibling)
        total = total + z_in[source].astype(F32)
    out_ref[...] = total.astype(BF16)
    for copy in open_copies:
        copy.wait_send()
    for k in range(1, 4):
        to = lax.rem(me.zl + k, 4)
        pltpu.make_async_remote_copy(
            src_ref=z_out.at[to // 2, to % 2], dst_ref=z_in.at[me.zl], send_sem=z_send.at[to],
            recv_sem=z_recv.at[me.zl], device_id=me.wide_peer(0, k, 0), device_id_type=MESH,
        ).wait_send()


def output(att, units, w_out, w_down, hidden, bias):
    width = hidden.shape[1]
    return pl.pallas_call(
        output_kernel,
        out_shape=jax.ShapeDtypeStruct(hidden.shape, BF16),
        in_specs=[pl.BlockSpec(memory_space=VM)] * 6,
        out_specs=pl.BlockSpec(memory_space=VM),
        scratch_shapes=[
            VM((8, 2, 2, 64, width), BF16),
            VM((8, 2, 64, width), BF16),
            VM((2, 4, 2, 64, width), BF16),
            VM((2, 3, 2, 64, width), BF16),
            VM((2, 2, 64, width), BF16),
            VM((4, 64, width), BF16),
            DMA((16,)),
            DMA((16,)),
            DMA((6,)),
            DMA((6,)),
            DMA((4,)),
            DMA((4,)),
        ],
        compiler_params=pltpu.CompilerParams(
            collective_id=1, has_side_effects=True, vmem_limit_bytes=56 << 20
        ),
        name="output",
    )(att, units, w_out, w_down, hidden, bias)


def local(
    hidden_in,
    w_query,
    w_key,
    w_value,
    qkv_bias,
    w_up,
    up_bias,
    w_attn_out,
    w_down,
    out_bias,
    norm_gain,
    norm_bias,
    seq_lens,
    sink_count,
    page_table,
):
    vmem = pl.BlockSpec(memory_space=VM)
    smem = pl.BlockSpec(memory_space=pltpu.SMEM)
    both = (QKV_PAD, QKV_PAD, UNITS, UNITS)
    qkv, units = pl.pallas_call(
        project_kernel,
        out_shape=[jax.ShapeDtypeStruct((TOKENS // OWN, OWN, c), BF16) for c in (QKV_PAD, UNITS)],
        in_specs=[smem] + [vmem] * 9,
        out_specs=[vmem] * 2,
        scratch_shapes=[
            VM((FEAT, QKV_PAD), BF16),
            VM((32, BLOCK, FEAT), BF16),
            VM((32, 8, 128), F32),
            VM((8, 8, 128), F32),
            VM((2, 3, OWN, ROT_COLS), F32),
            VM((2, 2, 8, 2, BLOCK, FEAT), BF16),
        ]
        + [VM((8, OWN, c), BF16) for c in both]
        + [VM((2, 2, OWN // 2, c), BF16) for c in both]
        + [VM((2, 2, OWN, c), BF16) for c in both]
        + [VM((2, OWN, c), BF16) for c in both]
        + [
            DMA((31,)),
            DMA((32,)),
            DMA((31,)),
            DMA((32,)),
            DMA((7,)),
            DMA((8,)),
            DMA((4, 22)),
            DMA((4, 22)),
        ],
        compiler_params=pltpu.CompilerParams(
            collective_id=0, has_side_effects=True, vmem_limit_bytes=56 << 20
        ),
        name="project",
    )(
        seq_lens,
        hidden_in,
        norm_gain,
        norm_bias,
        w_query.T,
        w_key.T,
        w_value.T,
        w_up,
        qkv_bias,
        up_bias,
    )
    slot_ids = lax.axis_index("narrow") * 16 + jnp.arange(16, dtype=jnp.int32)
    matches = (page_table[None, :] == slot_ids[:, None]).astype(jnp.int32)
    source_page = jnp.sum(matches * jnp.arange(NPAGES, dtype=jnp.int32)[None, :], axis=1)
    attended, cache = attend(seq_lens, sink_count, source_page, qkv.reshape(TOKENS, QKV_PAD), HEADS2)
    hidden_out = output(
        attended.reshape(8, 2 * OWN, HEADS2), units.reshape(8, 2 * OWN, UNITS), w_attn_out, w_down, hidden_in, out_bias
    )
    return (hidden_out, cache)


def solution(mesh):
    in_specs = (
        P("wide", "narrow"),
        P("narrow", "wide"),
        P("narrow", "wide"),
        P("narrow", "wide"),
        P(None, "wide"),
        P("narrow", "wide"),
        P("wide"),
        P("wide", "narrow"),
        P("wide", "narrow"),
        P("narrow"),
        P(None, "narrow"),
        P(None, "narrow"),
        P(),
        P(),
        P(),
    )
    out_specs = (P("wide", "narrow"), P(None, "narrow", None, "wide"))
    return jax.shard_map(local, mesh=mesh, in_specs=in_specs, out_specs=out_specs, check_vma=False)
```
